1024 devices in a mesh: node: 32 (over y, z_hi), local: 32 (over x, z_lo, core).
Axes of the slice: x: 4, y: 8, z: 16 (z_hi: 4, z_lo: 4; z = z_hi * 4 + z_lo), core: 2. Of those that a mesh axis runs over, the one named last changes fastest.
Arguments:
- tok_x: bfloat16 [2048, 2048], P(('node', 'local')), may hold values from -6 to 6
- grad_out: bfloat16 [2048, 2048], P(('node', 'local')), may hold values from -6 to 6
- expert_ids: int32 [2048, 8], P('node'), may hold values from 0 to 127, as said below
- slot_ids: int32 [2048, 8], P('node'), may hold values from 0 to 63, as said below
- route_probs: bfloat16 [2048, 8], P('node'), may hold values from 0.099609375 to 1
- gate_weight: bfloat16 [1024, 96, 2048], P(('node', 'local')), may hold values from -0.125 to 0.125
- up_weight: bfloat16 [1024, 96, 2048], P(('node', 'local')), may hold values from -0.125 to 0.125
- down_weight: bfloat16 [1024, 96, 2048], P(('node', 'local')), may hold values from -0.21875 to 0.21875
Outputs:
- grad_x: bfloat16 [2048, 2048], P(('node', 'local'))
- grad_probs: float32 [2048, 8], P(('node', 'local'))
- grad_gate: float32 [1024, 96, 2048], P(('node', 'local'))
- grad_up: float32 [1024, 96, 2048], P(('node', 'local'))
- grad_down: float32 [1024, 96, 2048], P(('node', 'local'))
The draws below stay inside these ranges and needn't reach their ends.
Inputs may be any that keep to these rules, and one draw needn't show every extreme that they name: `expert_ids`: each token names 8 different experts. Among the 64 tokens of every index of node, some expert is named by all 64 tokens. `slot_ids`: the pairs of the 64 tokens of one index of node that name one expert carry the slots 0, 1, 2 and so on, each once.
All inputs are finite; a program needn't handle non-finite values.
Results may differ from the reference program's by a relative error of at most 0.0049.
Values may be sent and summed in bfloat16 or wider, within the bound.
No kernel may reach another device: no remote copies, remote signals or barrier semaphores. Data moves between devices by JAX's collectives and lax.ppermute only.
A program may use at most 32 MiB of HBM per device.

```python
import math
import jax
import jax.numpy as jnp
from jax import lax

D = 2048
FF = 768
TOPK = 8
EXPERTS = 128
OWN = 8
HID_DEV = 96
NODE_TOK = 64
TOKENS = 2048
CAPN = 7
CAPE = 224


def slot_ranks(items):
    order_keys, experts_row = items
    same_expert = experts_row[None, :] == experts_row[:, None]
    earlier = order_keys[None, :] < order_keys[:, None]
    return jnp.sum((same_expert & earlier).astype(jnp.int32), axis=1).astype(jnp.int32)


def routing_table(key):
    base = jax.random.fold_in(key, 11)
    key_score = jax.random.fold_in(base, 0)
    key_favour = jax.random.fold_in(base, 1)
    key_hot = jax.random.fold_in(base, 2)
    key_order = jax.random.fold_in(base, 4)
    groups = TOKENS // NODE_TOK
    scores = jax.random.randint(key_score, (groups, NODE_TOK, EXPERTS), 0, 1 << 20)
    favour = jax.random.randint(key_favour, (groups, 1, EXPERTS), 0, 1 << 19)
    scores = scores + favour
    hottest = jax.random.randint(key_hot, (groups, 1, 1), 0, EXPERTS)
    forced = jnp.arange(EXPERTS, dtype=jnp.int32)[None, None, :] == hottest
    forced = jnp.broadcast_to(forced, (groups, NODE_TOK, EXPERTS))
    scores = jnp.where(forced, 1 << 21, scores)
    distinct = scores * EXPERTS + jnp.arange(EXPERTS, dtype=jnp.int32)[None, None, :]
    unused, chosen = lax.top_k(distinct, TOPK)
    chosen = chosen.astype(jnp.int32)
    pair_total = NODE_TOK * TOPK
    order_keys = jax.random.randint(key_order, (groups, pair_total), 0, 1 << 16) * pair_total + jnp.arange(pair_total, dtype=jnp.int32)[None, :]
    slots = lax.map(slot_ranks, (order_keys, chosen.reshape(groups, pair_total)))
    return (chosen.reshape(TOKENS, TOPK), slots.reshape(TOKENS, TOPK).astype(jnp.int32))


def draw_expert_ids(key, part):
    experts_all, slots_all = routing_table(key)
    return experts_all


def draw_slot_ids(key, part):
    experts_all, slots_all = routing_table(key)
    return slots_all


def level_of(key, extent, shards, low, high):
    level, own = 1.0, jax.random.fold_in(key, 6)
    for axis_at, shards_of in shards:
        steps = jnp.exp(jax.random.uniform(jax.random.fold_in(own, axis_at), (shards_of,), jnp.float32, low / len(shards), high / len(shards)))
        level = level * jnp.repeat(steps, extent[axis_at] // shards_of).reshape([-1 if axis == axis_at else 1 for axis in range(len(extent))])
    return level


def bell_draw(own_key, dims, scale, limit, cuts=(), kind=jnp.bfloat16):
    drawn = jax.random.normal(own_key, dims, jnp.float32) * scale
    if len(cuts) > 0:
        drawn = level_of(own_key, dims, cuts, -0.22, 0.18) * drawn
    return jnp.clip(drawn, min=-limit, max=limit).astype(kind)


def setup_inputs(seed: int = 0) -> dict:
    arg_keys = jax.random.split(jax.random.key(seed), 9)
    return {
        "tok_x": bell_draw(arg_keys[0], (TOKENS, D), 1.0, 6.0, ((0, 1024),)),
        "grad_out": bell_draw(arg_keys[1], (TOKENS, D), 1.0, 6.0, ((0, 1024),)),
        "expert_ids": draw_expert_ids(jax.random.fold_in(arg_keys[8], 71), 0),
        "slot_ids": draw_slot_ids(jax.random.fold_in(arg_keys[8], 71), 0),
        "route_probs": jnp.clip(jnp.exp(math.log(1.0) - 2.306499 * jax.random.uniform(arg_keys[4], (TOKENS, TOPK), jnp.float32) ** level_of(arg_keys[4], (TOKENS, TOPK), ((0, 32),), -0.2, 0.2)), 0.099609375, 1.0).astype(jnp.bfloat16),
        "gate_weight": bell_draw(arg_keys[5], (EXPERTS * OWN, HID_DEV, D), D ** -0.5, 0.125, ((0, 1024),)),
        "up_weight": bell_draw(arg_keys[6], (EXPERTS * OWN, HID_DEV, D), D ** -0.5, 0.125, ((0, 1024),)),
        "down_weight": bell_draw(arg_keys[7], (EXPERTS * OWN, HID_DEV, D), FF ** -0.5, 0.21875, ((0, 1024),)),
    }


def expert_grads(rows_x, rows_d, rows_p, w_gate_e, w_up_e, w_down_e):
    gate_pre = jnp.dot(rows_x, w_gate_e.T, preferred_element_type=jnp.float32)
    up_pre = jnp.dot(rows_x, w_up_e.T, preferred_element_type=jnp.float32)
    sigmoid_gate = jax.nn.sigmoid(gate_pre)
    activated = gate_pre * sigmoid_gate
    hidden = activated * up_pre
    back_proj = jnp.dot(rows_d, w_down_e.T, preferred_element_type=jnp.float32)
    pair_grad = jnp.sum(hidden * back_proj, axis=1)
    d_hidden = rows_p[:, None] * back_proj
    d_gate = (d_hidden * up_pre * sigmoid_gate * (1.0 + gate_pre * (1.0 - sigmoid_gate))).astype(jnp.bfloat16)
    d_up = (d_hidden * activated).astype(jnp.bfloat16)
    scaled_hidden = (rows_p[:, None] * hidden).astype(jnp.bfloat16)
    input_grad = jnp.dot(d_gate, w_gate_e, preferred_element_type=jnp.float32) + jnp.dot(d_up, w_up_e, preferred_element_type=jnp.float32)
    gate_grad = jnp.dot(d_gate.T, rows_x, preferred_element_type=jnp.float32)
    up_grad = jnp.dot(d_up.T, rows_x, preferred_element_type=jnp.float32)
    down_grad = jnp.dot(scaled_hidden.T, rows_d, preferred_element_type=jnp.float32)
    return input_grad, pair_grad, gate_grad, up_grad, down_grad


def reference(tok_x, grad_out, expert_ids, slot_ids, route_probs, gate_weight, up_weight, down_weight):
    pair_count = TOKENS * TOPK
    flat_expert = expert_ids.reshape(-1).astype(jnp.int32)
    flat_slot = slot_ids.reshape(-1).astype(jnp.int32)
    pair_ids = jnp.arange(pair_count, dtype=jnp.int32)
    group_ids = (pair_ids // (TOPK * NODE_TOK)).astype(jnp.int32)
    is_kept = flat_slot < CAPN
    target = jnp.where(is_kept, flat_expert * CAPE + group_ids * CAPN + flat_slot, EXPERTS * CAPE).astype(jnp.int32)
    slot_table = jnp.full((EXPERTS * CAPE,), pair_count, dtype=jnp.int32).at[target].set(pair_ids, mode="drop")
    slot_table = slot_table.reshape(EXPERTS, CAPE)
    flat_probs = route_probs.reshape(-1).astype(jnp.float32)
    gate_all = gate_weight.reshape(EXPERTS, FF, D)
    up_all = up_weight.reshape(EXPERTS, FF, D)
    down_all = down_weight.reshape(EXPERTS, FF, D)

    def one_expert(items):
        table_row, w_gate_e, w_up_e, w_down_e = items
        token_rows = (table_row // TOPK).astype(jnp.int32)
        rows_x = jnp.take(tok_x, token_rows, axis=0, mode="fill", fill_value=0)
        rows_d = jnp.take(grad_out, token_rows, axis=0, mode="fill", fill_value=0)
        rows_p = jnp.take(flat_probs, table_row, mode="fill", fill_value=0)
        return expert_grads(rows_x, rows_d, rows_p, w_gate_e, w_up_e, w_down_e)

    input_grad, pair_grad, gate_grad, up_grad, down_grad = lax.map(one_expert, (slot_table, gate_all, up_all, down_all))
    all_rows = (slot_table // TOPK).reshape(-1).astype(jnp.int32)
    grad_x = jnp.zeros((TOKENS, D), jnp.float32).at[all_rows].add(input_grad.reshape(-1, D), mode="drop")
    grad_probs = jnp.zeros((pair_count,), jnp.float32).at[slot_table.reshape(-1)].add(pair_grad.reshape(-1), mode="drop")
    return (grad_x.astype(jnp.bfloat16), grad_probs.reshape(TOKENS, TOPK), gate_grad.reshape(EXPERTS * OWN, HID_DEV, D), up_grad.reshape(EXPERTS * OWN, HID_DEV, D), down_grad.reshape(EXPERTS * OWN, HID_DEV, D))
```

```python
import jax
import jax.numpy as jnp
from jax import lax
from jax.experimental import pallas as pl
from jax.experimental.pallas import tpu as pltpu
from jax.sharding import PartitionSpec as P

NODES = 32
CLASSES = 4
ZL = 4
CORES = 2
COLS = ZL * CORES
CAPN = 7
SLOTS = 8
ROWS = NODES * SLOTS
TOPK = 8
TOK = 64
D = 2048
CB = D // COLS
HID = 96
LANES = 128
BF = jnp.bfloat16
F32 = jnp.float32

NT = (((1,), (1,)), ((), ()))
NN = (((1,), (0,)), ((), ()))
TN = (((0,), (0,)), ((), ()))


def dot(a, b, dims):
    return lax.dot_general(a, b, dims, preferred_element_type=F32)


def shift_pairs(step):
    return [
        (x * COLS + z * CORES + c, x * COLS + ((z + step) % ZL) * CORES + c)
        for x in range(CLASSES)
        for z in range(ZL)
        for c in range(CORES)
    ]


CORE_PAIRS = [(i, i ^ 1) for i in range(CLASSES * COLS)]


def targets(ids, slots, own_class):
    keep = ((ids & (CLASSES - 1)) == own_class) & (slots < CAPN)
    return jnp.where(keep, (ids >> 2) * SLOTS + slots, -1)


def row_iotas():
    lane = lax.broadcasted_iota(jnp.int32, (ROWS, LANES), 1)
    sub = lax.broadcasted_iota(jnp.int32, (ROWS, LANES), 0) & (SLOTS - 1)
    return lane, sub


def spread_column(column):
    lane, sub = row_iotas()
    put = jnp.where(lane == sub, column, 0.0).reshape(NODES, SLOTS, LANES)
    group = jnp.sum(put, axis=1, keepdims=True)
    return jnp.broadcast_to(group, (NODES, SLOTS, LANES)).reshape(ROWS, LANES)


def gather_column(block):
    lane, sub = row_iotas()
    last = block.reshape(NODES, SLOTS, LANES)[:, SLOTS - 1 :, :]
    last = jnp.broadcast_to(last, (NODES, SLOTS, LANES)).reshape(ROWS, LANES)
    return jnp.sum(jnp.where(lane == sub, last, 0.0), axis=1, keepdims=True)


def spread_kernel(x_ref, d_ref, out_ref):
    for j in range(COLS):
        cols = pl.ds(j * CB, CB)
        for c in range(CLASSES):
            out_ref[c * COLS + j, :, :CB] = x_ref[:, cols]
            out_ref[c * COLS + j, :, CB:] = d_ref[:, cols]


def route_kernel(where_ref, ids_ref, slots_ref, probs_ref, hits_ref, weight_ref, pick_ref):
    target = targets(ids_ref[...], slots_ref[...], where_ref[0])
    probs = probs_ref[...].astype(F32)
    row = lax.broadcasted_iota(jnp.int32, (ROWS, TOK), 0)
    hits = jnp.zeros((ROWS, TOK), F32)
    weight = jnp.zeros((ROWS, TOK), F32)
    choice = jnp.zeros((ROWS, TOK), F32)
    for k in range(TOPK):
        hit = row == target[k : k + 1, :]
        hits = jnp.where(hit, 1.0, hits)
        weight = jnp.where(hit, probs[k : k + 1, :], weight)
        choice = jnp.where(hit, float(k), choice)
    lane, sub = row_iotas()
    hits_ref[...] = hits.astype(BF)
    group = spread_column(jnp.sum(weight, axis=1, keepdims=True))
    weight_ref[...] = jnp.where(sub == SLOTS - 1, group, 0.0).astype(BF)
    pick = jnp.sum(choice, axis=1, keepdims=True).astype(jnp.int32)
    pick_ref[...] = jnp.where(lane == pick, 1.0, 0.0).astype(BF)


def dispatch_kernel(hits_ref, weight_ref, tok_ref, out_ref):
    rows = dot(hits_ref[...], tok_ref[...].reshape(TOK, 2 * CB), NN)
    out_ref[:, :LANES] = (rows[:, :LANES] + weight_ref[...].astype(F32)).astype(BF)
    out_ref[:, LANES:] = rows[:, LANES:].astype(BF)


def block_starts(where_ref):
    z, core = where_ref[1], where_ref[2]
    starts = []
    for side in range(CORES):
        c = core if side == 0 else 1 - core
        for step in range(ZL):
            owner = ((z - step + ZL) & (ZL - 1)) * CORES + c
            starts.append(pl.multiple_of(owner * CB, CB))
    return starts


def store_input_grads(out_ref, starts, d_gate, d_up, pair, wg, wu):
    _, sub = row_iotas()
    for i, start in enumerate(starts):
        cols = pl.ds(start, CB)
        out = dot(d_gate, wg[:, cols], NN) + dot(d_up, wu[:, cols], NN)
        head = jnp.where(sub == SLOTS - 1, pair, out[:, :LANES])
        out_ref[i, :, :LANES] = head.astype(out_ref.dtype)
        out_ref[i, :, LANES:] = out[:, LANES:].astype(out_ref.dtype)


def hidden_kernel(where_ref, *refs):
    blocks = refs[: 2 * ZL]
    wg, wu, wd = refs[2 * ZL : 2 * ZL + 3]
    other_ref, gate_ref, up_ref, pair_ref, grads_ref = refs[2 * ZL + 3 :]
    starts = block_starts(where_ref)
    gate = jnp.zeros((ROWS, HID), F32)
    up = jnp.zeros((ROWS, HID), F32)
    back = jnp.zeros((ROWS, HID), F32)
    for block, start in zip(blocks, starts, strict=True):
        cols = pl.ds(start, CB)
        gate += dot(block[:, :CB], wg[:, cols], NT)
        up += dot(block[:, :CB], wu[:, cols], NT)
        back += dot(block[:, CB:], wd[:, cols], NT)
    prob = gather_column(blocks[0][:, :LANES].astype(F32))
    sig = jax.nn.sigmoid(gate)
    act = gate * sig
    hidden = act * up
    pair = spread_column(jnp.sum(hidden * back, axis=1, keepdims=True))
    d_hidden = prob * back
    d_gate = d_hidden * up * sig * (1.0 + gate * (1.0 - sig))
    d_up = d_hidden * act
    scaled = prob * hidden
    grads_ref[0] = d_gate.T.astype(BF)
    grads_ref[1] = d_up.T.astype(BF)
    grads_ref[2] = scaled.T.astype(BF)
    d_gate = d_gate.astype(BF)
    d_up = d_up.astype(BF)
    gate_ref[...] = d_gate
    up_ref[...] = d_up
    pair_ref[...] = pair
    store_input_grads(other_ref, starts[ZL:], d_gate, d_up, pair, wg, wu)


def own_kernel(where_ref, gate_ref, up_ref, pair_ref, wg, wu, out_ref):
    starts = block_starts(where_ref)[:ZL]
    store_input_grads(out_ref, starts, gate_ref[...], up_ref[...], pair_ref[...], wg, wu)


def weight_kernel(where_ref, *refs):
    blocks = refs[: 2 * ZL]
    grads_ref = refs[2 * ZL]
    gate_ref, up_ref, down_ref = refs[2 * ZL + 1 :]
    for block, start in zip(blocks, block_starts(where_ref), strict=True):
        cols = pl.ds(start, CB)
        gate_ref[:, cols] = dot(grads_ref[0], block[:, :CB], NN)
        up_ref[:, cols] = dot(grads_ref[1], block[:, :CB], NN)
        down_ref[:, cols] = dot(grads_ref[2], block[:, CB:], NN)


def combine_kernel(hits_ref, pick_ref, back_ref, out_ref):
    hits = hits_ref[...]
    value = gather_column(back_ref[:, :LANES].astype(F32))
    pairs = (pick_ref[...].astype(F32) * value).astype(BF)
    rows = dot(hits, back_ref[...], TN)
    probs = dot(hits, pairs, TN)
    for i in range(CLASSES * COLS):
        out_ref[i, :, :CB] = rows[2 * i : 2 * i + 2]
        out_ref[i, :, CB:] = probs[2 * i : 2 * i + 2]


def finish_kernel(in_ref, x_ref, p_ref):
    for j in range(COLS):
        total = in_ref[j]
        for c in range(1, CLASSES):
            total += in_ref[c * COLS + j]
        x_ref[:, j * CB : (j + 1) * CB] = total[:, :CB].astype(BF)
        if j == 0:
            p_ref[...] = total[:, CB : CB + TOPK]


VMEM_LIMIT = 16 << 20


def call(kernel, args, outs, scalars=None, near=True, flops=0, moved=0):
    vmem = pl.BlockSpec(memory_space=pltpu.VMEM)
    smem = pl.BlockSpec(memory_space=pltpu.SMEM)
    if near:
        args = [pltpu.with_memory_space_constraint(v, pltpu.VMEM) for v in args]
    in_specs = [vmem] * len(args)
    if scalars is not None:
        args, in_specs = [scalars, *args], [smem, *in_specs]
    return pl.pallas_call(
        kernel,
        out_shape=outs,
        in_specs=in_specs,
        out_specs=jax.tree.map(lambda _: vmem, outs, is_leaf=lambda v: hasattr(v, "dtype")),
        compiler_params=pltpu.CompilerParams(vmem_limit_bytes=VMEM_LIMIT),
        cost_estimate=pl.CostEstimate(flops=flops, bytes_accessed=moved, transcendentals=0),
    )(*args)


def shape(dims, dtype):
    return jax.ShapeDtypeStruct(dims, dtype)


def near(dims, dtype):
    return pltpu.VMEM(dims, dtype)


def exchange(v, axis):
    return lax.all_to_all(v, axis, split_axis=0, concat_axis=0, tiled=True)


def local(tok_x, grad_out, expert_ids, slot_ids, route_probs, gate_weight, up_weight, down_weight):
    place = lax.axis_index("local")
    where = jnp.stack([place // COLS, (place // CORES) % ZL, place % CORES]).astype(jnp.int32)
    wg, wu, wd = gate_weight[0], up_weight[0], down_weight[0]
    own = tok_x.shape[0]
    peers = CLASSES * COLS
    with jax.named_scope("tokens_to_columns"):
        both = call(spread_kernel, [tok_x, grad_out], near((peers, own, 2 * CB), BF))
        tokens = exchange(both, "local")
    with jax.named_scope("routing"):
        hits, weight, pick = call(
            route_kernel,
            [expert_ids.T, slot_ids.T, route_probs.T],
            (near((ROWS, TOK), BF), near((ROWS, LANES), BF), near((ROWS, LANES), BF)),
            scalars=where,
        )
    with jax.named_scope("rows_to_experts"):
        outbox = call(dispatch_kernel, [hits, weight, tokens], near((ROWS, 2 * CB), BF))
        rows = exchange(outbox.reshape(NODES, SLOTS, 2 * CB), "node").reshape(ROWS, 2 * CB)
    with jax.named_scope("gather_columns"):
        mine = [rows] + [
            lax.ppermute(rows, "local", shift_pairs(step)) for step in range(1, ZL)
        ]
        theirs = [lax.ppermute(v, "local", CORE_PAIRS) for v in mine]
    blocks = mine + theirs
    with jax.named_scope("hidden_grads"):
        other, d_gate, d_up, pair, grads = call(
            hidden_kernel,
            [*blocks, wg, wu, wd],
            (
                near((ZL, ROWS, CB), BF),
                near((ROWS, HID), BF),
                near((ROWS, HID), BF),
                near((ROWS, LANES), F32),
                shape((3, HID, ROWS), BF),
            ),
            scalars=where,
            flops=8 * ROWS * HID * D,
            moved=4 << 20,
        )
    with jax.named_scope("scatter_columns"):
        other = lax.ppermute(other, "local", CORE_PAIRS)
        part = call(
            own_kernel,
            [d_gate, d_up, pair, wg, wu],
            near((ZL, ROWS, CB), F32),
            scalars=where,
            flops=2 * ROWS * HID * D,
            moved=2 << 20,
        )
        sums = [part[step] + other[step].astype(F32) for step in range(ZL)]
        moved = [
            lax.ppermute(sums[step].astype(BF), "local", shift_pairs(-step))
            for step in range(1, ZL)
        ]
    with jax.named_scope("weight_grads"):
        weight_grads = call(
            weight_kernel,
            [*blocks, grads],
            (shape((HID, D), F32),) * 3,
            scalars=where,
            near=False,
            flops=6 * ROWS * HID * D,
            moved=5 << 20,
        )
    moved, weight_grads = lax.optimization_barrier((moved, weight_grads))
    with jax.named_scope("rows_to_tokens"):
        total = sums[0]
        for v in moved:
            total += v.astype(F32)
        back = exchange(total.astype(BF).reshape(NODES, SLOTS, CB), "node").reshape(ROWS, CB)
        partial = call(combine_kernel, [hits, pick, back], near((peers, own, CB + LANES), F32))
    with jax.named_scope("columns_to_tokens"):
        pieces = exchange(partial, "local")
        grad_x, grad_p = call(finish_kernel, [pieces], (shape((own, D), BF), shape((own, TOPK), F32)))
    gate_grad, up_grad, down_grad = weight_grads
    return grad_x, grad_p, gate_grad[None], up_grad[None], down_grad[None]


def solution(mesh):
    both = ("node", "local")
    in_specs = (
        P(both, None),
        P(both, None),
        P("node", None),
        P("node", None),
        P("node", None),
        P(both, None, None),
        P(both, None, None),
        P(both, None, None),
    )
    out_specs = (
        P(both, None),
        P(both, None),
        P(both, None, None),
        P(both, None, None),
        P(both, None, None),
    )
    return jax.shard_map(local, mesh=mesh, in_specs=in_specs, out_specs=out_specs, check_vma=False)
```

```python
import jax
import jax.numpy as jnp
from jax import lax
from jax.experimental import pallas as pl
from jax.experimental.pallas import tpu as pltpu
from jax.sharding import PartitionSpec as P

NODES = 32
CLASSES = 4
ZL = 4
CORES = 2
COLS = ZL * CORES
CAPN = 7
SLOTS = 8
ROWS = NODES * SLOTS
TOPK = 8
TOK = 64
D = 2048
CB = D // COLS
HID = 96
PAIR = CORES * HID
PRE = 640
LANES = 128
BF = jnp.bfloat16
F32 = jnp.float32

NT = (((1,), (1,)), ((), ()))
NN = (((1,), (0,)), ((), ()))
TN = (((0,), (0,)), ((), ()))


def dot(a, b, dims):
    return lax.dot_general(a, b, dims, preferred_element_type=F32)


def shift_pairs(step):
    return [
        (x * COLS + z * CORES + c, x * COLS + ((z + step) % ZL) * CORES + c)
        for x in range(CLASSES)
        for z in range(ZL)
        for c in range(CORES)
    ]


CORE_PAIRS = [(i, i ^ 1) for i in range(CLASSES * COLS)]


def targets(ids, slots, own_class):
    keep = ((ids & (CLASSES - 1)) == own_class) & (slots < CAPN)
    return jnp.where(keep, (ids >> 2) * SLOTS + slots, -1)


def row_iotas():
    lane = lax.broadcasted_iota(jnp.int32, (ROWS, LANES), 1)
    sub = lax.broadcasted_iota(jnp.int32, (ROWS, LANES), 0) & (SLOTS - 1)
    return lane, sub


def spread_column(column):
    lane, sub = row_iotas()
    put = jnp.where(lane == sub, column, 0.0).reshape(NODES, SLOTS, LANES)
    group = jnp.sum(put, axis=1, keepdims=True)
    return jnp.broadcast_to(group, (NODES, SLOTS, LANES)).reshape(ROWS, LANES)


def gather_column(block):
    lane, sub = row_iotas()
    last = block.reshape(NODES, SLOTS, LANES)[:, SLOTS - 1 :, :]
    last = jnp.broadcast_to(last, (NODES, SLOTS, LANES)).reshape(ROWS, LANES)
    return jnp.sum(jnp.where(lane == sub, last, 0.0), axis=1, keepdims=True)


def spread_kernel(x_ref, d_ref, out_ref):
    for j in range(COLS):
        cols = pl.ds(j * CB, CB)
        for c in range(CLASSES):
            out_ref[c * COLS + j, :, :CB] = x_ref[:, cols]
            out_ref[c * COLS + j, :, CB:] = d_ref[:, cols]


def route_kernel(where_ref, ids_ref, slots_ref, probs_ref, hits_ref, weight_ref, pick_ref):
    target = targets(ids_ref[...], slots_ref[...], where_ref[0])
    probs = probs_ref[...].astype(F32)
    row = lax.broadcasted_iota(jnp.int32, (ROWS, TOK), 0)
    hits = jnp.zeros((ROWS, TOK), F32)
    weight = jnp.zeros((ROWS, TOK), F32)
    choice = jnp.zeros((ROWS, TOK), F32)
    for k in range(TOPK):
        hit = row == target[k : k + 1, :]
        hits = jnp.where(hit, 1.0, hits)
        weight = jnp.where(hit, probs[k : k + 1, :], weight)
        choice = jnp.where(hit, float(k), choice)
    lane, sub = row_iotas()
    hits_ref[...] = hits.astype(BF)
    group = spread_column(jnp.sum(weight, axis=1, keepdims=True))
    weight_ref[...] = jnp.where(sub == SLOTS - 1, group, 0.0).astype(BF)
    pick = jnp.sum(choice, axis=1, keepdims=True).astype(jnp.int32)
    pick_ref[...] = jnp.where(lane == pick, 1.0, 0.0).astype(BF)


def dispatch_kernel(hits_ref, weight_ref, tok_ref, out_ref):
    rows = dot(hits_ref[...], tok_ref[...].reshape(TOK, 2 * CB), NN)
    out_ref[:, :LANES] = (rows[:, :LANES] + weight_ref[...].astype(F32)).astype(BF)
    out_ref[:, LANES:] = rows[:, LANES:].astype(BF)


def block_starts(where_ref):
    z, core = where_ref[1], where_ref[2]
    starts = []
    for side in range(CORES):
        c = core if side == 0 else 1 - core
        for step in range(ZL):
            owner = ((z - step + ZL) & (ZL - 1)) * CORES + c
            starts.append(pl.multiple_of(owner * CB, CB))
    return starts


def core_starts(where_ref):
    z = where_ref[1]
    return [
        pl.multiple_of(((z - step + ZL) & (ZL - 1)) * CB, CB) for step in range(ZL)
    ]


def lend_kernel(where_ref, wg, wu, wd, out_ref):
    other = 1 - where_ref[2]
    for i, w in enumerate((wg, wu, wd)):
        for z in range(ZL):
            cols = pl.ds(pl.multiple_of((z * CORES + other) * CB, CB), CB)
            out_ref[i * HID : (i + 1) * HID, z * CB : (z + 1) * CB] = w[:, cols]


def stack_kernel(where_ref, wg, wu, wd, lent, into_ref, down_ref):
    core = where_ref[2]
    for i, (w, ref, base) in enumerate(
        ((wg, into_ref, 0), (wu, into_ref, PAIR), (wd, down_ref, 0))
    ):
        mine = pl.ds(pl.multiple_of(base + core * HID, HID // 3), HID)
        theirs = pl.ds(pl.multiple_of(base + (1 - core) * HID, HID // 3), HID)
        ref[theirs, :] = lent[i * HID : (i + 1) * HID, :]
        for z in range(ZL):
            cols = pl.ds(pl.multiple_of((z * CORES + core) * CB, CB), CB)
            ref[mine, z * CB : (z + 1) * CB] = w[:, cols]


def partial_kernel(where_ref, *refs):
    blocks = refs[:ZL]
    into, down, out_ref, stacked_ref = refs[ZL:]
    first = jnp.zeros((ROWS, 2 * PAIR), F32)
    last = jnp.zeros((ROWS, PAIR), F32)
    for block, start in zip(blocks, core_starts(where_ref), strict=True):
        cols = pl.ds(start, CB)
        first += dot(block[:, :CB], into[:, cols], NT)
        last += dot(block[:, CB:], down[:, cols], NT)
    out_ref[:, : 2 * PAIR] = first
    out_ref[:, 2 * PAIR : 3 * PAIR] = last
    out_ref[:, 3 * PAIR :] = jnp.zeros((ROWS, PRE - 3 * PAIR), F32)
    for step, block in enumerate(blocks):
        stacked_ref[step] = block[...]


def hidden_kernel(where_ref, half_ref, other_ref, rows_ref, into, *outs):
    grads_ref, own_ref = outs[:2]
    pre = half_ref[...] + other_ref[...]
    gate, up, back = pre[:, :PAIR], pre[:, PAIR : 2 * PAIR], pre[:, 2 * PAIR : 3 * PAIR]
    prob = gather_column(rows_ref[:, :LANES].astype(F32))
    sig = jax.nn.sigmoid(gate)
    act = gate * sig
    hidden = act * up
    pair = spread_column(jnp.sum(hidden * back, axis=1, keepdims=True))
    d_hidden = prob * back
    d_gate = d_hidden * up * sig * (1.0 + gate * (1.0 - sig))
    d_up = d_hidden * act
    scaled = prob * hidden
    _, sub = row_iotas()
    gate_bf, up_bf = d_gate.astype(BF), d_up.astype(BF)
    for ref, start in zip((own_ref, *outs[2:]), core_starts(where_ref), strict=True):
        cols = pl.ds(start, CB)
        out = dot(gate_bf, into[:PAIR, cols], NN) + dot(up_bf, into[PAIR:, cols], NN)
        head = jnp.where(sub == SLOTS - 1, pair, out[:, :LANES])
        ref[:, :LANES] = head.astype(ref.dtype)
        ref[:, LANES:] = out[:, LANES:].astype(ref.dtype)
    grads_ref[0] = d_gate.T.astype(BF)
    grads_ref[1] = d_up.T.astype(BF)
    grads_ref[2] = scaled.T.astype(BF)


def weight_kernel(where_ref, *refs):
    blocks = [*refs[:ZL], *(refs[ZL].at[step] for step in range(ZL))]
    grads_ref, gate_ref, up_ref, down_ref = refs[ZL + 1 :]
    mine = pl.ds(pl.multiple_of(where_ref[2] * HID, HID // 3), HID)
    d_gate, d_up, scaled = (grads_ref[i, mine, :] for i in range(3))
    for block, start in zip(blocks, block_starts(where_ref), strict=True):
        cols = pl.ds(start, CB)
        gate_ref[:, cols] = dot(d_gate, block[:, :CB], NN)
        up_ref[:, cols] = dot(d_up, block[:, :CB], NN)
        down_ref[:, cols] = dot(scaled, block[:, CB:], NN)


def combine_kernel(hits_ref, pick_ref, back_ref, out_ref):
    hits = hits_ref[...]
    value = gather_column(back_ref[:, :LANES].astype(F32))
    pairs = (pick_ref[...].astype(F32) * value).astype(BF)
    rows = dot(hits, back_ref[...], TN)
    probs = dot(hits, pairs, TN)
    for i in range(CLASSES * COLS):
        out_ref[i, :, :CB] = rows[2 * i : 2 * i + 2]
        out_ref[i, :, CB:] = probs[2 * i : 2 * i + 2]


def finish_kernel(in_ref, x_ref, p_ref):
    for j in range(COLS):
        total = in_ref[j]
        for c in range(1, CLASSES):
            total += in_ref[c * COLS + j]
        x_ref[:, j * CB : (j + 1) * CB] = total[:, :CB].astype(BF)
        if j == 0:
            p_ref[...] = total[:, CB : CB + TOPK]


VMEM_LIMIT = 16 << 20


def call(kernel, args, outs, scalars=None, inside=True, flops=0, moved=0):
    vmem = pl.BlockSpec(memory_space=pltpu.VMEM)
    smem = pl.BlockSpec(memory_space=pltpu.SMEM)
    if inside is not None:
        space = pltpu.VMEM if inside else pltpu.HBM
        args = [pltpu.with_memory_space_constraint(v, space) for v in args]
    in_specs = [vmem] * len(args)
    if scalars is not None:
        args, in_specs = [scalars, *args], [smem, *in_specs]
    return pl.pallas_call(
        kernel,
        out_shape=outs,
        in_specs=in_specs,
        out_specs=jax.tree.map(lambda _: vmem, outs, is_leaf=lambda v: hasattr(v, "dtype")),
        compiler_params=pltpu.CompilerParams(vmem_limit_bytes=VMEM_LIMIT),
        cost_estimate=pl.CostEstimate(flops=flops, bytes_accessed=moved, transcendentals=0),
    )(*args)


def shape(dims, dtype):
    return jax.ShapeDtypeStruct(dims, dtype)


def near(dims, dtype):
    return pltpu.VMEM(dims, dtype)


def exchange(v, axis):
    return lax.all_to_all(v, axis, split_axis=0, concat_axis=0, tiled=True)


def local(tok_x, grad_out, expert_ids, slot_ids, route_probs, gate_weight, up_weight, down_weight):
    place = lax.axis_index("local")
    where = jnp.stack([place // COLS, (place // CORES) % ZL, place % CORES]).astype(jnp.int32)
    wg, wu, wd = gate_weight[0], up_weight[0], down_weight[0]
    own = tok_x.shape[0]
    peers = CLASSES * COLS
    with jax.named_scope("tokens_to_columns"):
        both = call(spread_kernel, [tok_x, grad_out], near((peers, own, 2 * CB), BF), inside=False)
        tokens = exchange(both, "local")
    with jax.named_scope("routing"):
        hits, weight, pick = call(
            route_kernel,
            [expert_ids.T, slot_ids.T, route_probs.T],
            (near((ROWS, TOK), BF), near((ROWS, LANES), BF), near((ROWS, LANES), BF)),
            scalars=where,
        )
    with jax.named_scope("core_weights"):
        lent = call(lend_kernel, [wg, wu, wd], near((3 * HID, ZL * CB), BF), scalars=where)
        lent = lax.ppermute(lent, "local", CORE_PAIRS)
        into, down = call(
            stack_kernel,
            [wg, wu, wd, lent],
            (near((2 * PAIR, ZL * CB), BF), near((PAIR, ZL * CB), BF)),
            scalars=where,
        )
    with jax.named_scope("rows_to_experts"):
        outbox = call(dispatch_kernel, [hits, weight, tokens], near((ROWS, 2 * CB), BF))
        rows = exchange(outbox.reshape(NODES, SLOTS, 2 * CB), "node").reshape(ROWS, 2 * CB)
    with jax.named_scope("gather_columns"):
        mine = [rows] + [
            lax.ppermute(rows, "local", shift_pairs(step)) for step in range(1, ZL)
        ]
    with jax.named_scope("hidden_grads"):
        half, stacked = call(
            partial_kernel,
            [*mine, into, down],
            (near((ROWS, PRE), F32), near((ZL, ROWS, 2 * CB), BF)),
            scalars=where,
            flops=6 * ROWS * HID * D,
            moved=3 << 20,
        )
        other = lax.ppermute(half, "local", CORE_PAIRS)
        grads, total, *sums = call(
            hidden_kernel,
            [half, other, rows, into],
            (shape((3, PAIR, ROWS), BF), near((ROWS, CB), F32)) + (near((ROWS, CB), BF),) * (ZL - 1),
            scalars=where,
            flops=4 * ROWS * HID * D,
            moved=2 << 20,
        )
    with jax.named_scope("scatter_columns"):
        moved = [
            lax.ppermute(v, "local", shift_pairs(-step)) for step, v in enumerate(sums, start=1)
        ]
        stacked, sums = lax.optimization_barrier((stacked, sums))
        theirs = lax.ppermute(stacked, "local", CORE_PAIRS)
    with jax.named_scope("weight_grads"):
        weight_grads = call(
            weight_kernel,
            [*mine, theirs, grads],
            (shape((HID, D), F32),) * 3,
            scalars=where,
            inside=None,
            flops=6 * ROWS * HID * D,
            moved=5 << 20,
        )
    moved, weight_grads = lax.optimization_barrier((moved, weight_grads))
    with jax.named_scope("rows_to_tokens"):
        for v in moved:
            total += v.astype(F32)
        back = exchange(total.astype(BF).reshape(NODES, SLOTS, CB), "node").reshape(ROWS, CB)
        partial = call(combine_kernel, [hits, pick, back], near((peers, own, CB + LANES), F32))
    with jax.named_scope("columns_to_tokens"):
        pieces = exchange(partial, "local")
        grad_x, grad_p = call(finish_kernel, [pieces], (shape((own, D), BF), shape((own, TOPK), F32)))
    gate_grad, up_grad, down_grad = weight_grads
    return grad_x, grad_p, gate_grad[None], up_grad[None], down_grad[None]


def solution(mesh):
    both = ("node", "local")
    in_specs = (
        P(both, None),
        P(both, None),
        P("node", None),
        P("node", None),
        P("node", None),
        P(both, None, None),
        P(both, None, None),
        P(both, None, None),
    )
    out_specs = (
        P(both, None),
        P(both, None),
        P(both, None, None),
        P(both, None, None),
        P(both, None, None),
    )
    return jax.shard_map(local, mesh=mesh, in_specs=in_specs, out_specs=out_specs, check_vma=False)
```
